256 devices in a mesh: wide: 16 (over y, x), narrow: 16 (over z, core).
Axes of the slice: x: 4, y: 4, z: 8, core: 2. Of those that a mesh axis runs over, the one named last changes fastest.
Arguments:
- messages: bfloat16 [393216, 512], P(('wide', 'narrow')), may hold values from -6 to 6
- reverse_position: int32 [393216], P(('wide', 'narrow')), may hold values from 0 to 95, as said below
- route_slot: int32 [393216], P(('wide', 'narrow')), may hold values from 0 to 3071, as said below
- atom_slots: int32 [393216], P(('wide', 'narrow')), may hold values from 0 to 3071, as said below
- angles: bfloat16 [12288, 1024], P(('wide', 'narrow')), may hold values from -1 to 1
- weight_message: bfloat16 [2, 512, 512], replicated, may hold values from -0.25 to 0.25
- weight_reverse: bfloat16 [2, 512, 512], replicated, may hold values from -0.25 to 0.25
- weight_combine: bfloat16 [2, 512, 512], replicated, may hold values from -0.25 to 0.25
- weight_inner: bfloat16 [2, 512, 512], replicated, may hold values from -0.25 to 0.25
- weight_outer: bfloat16 [2, 512, 512], replicated, may hold values from -0.25 to 0.25
- weight_lift: bfloat16 [2, 512, 512], replicated, may hold values from -0.25 to 0.25
- weight_expand: bfloat16 [2, 512, 512], replicated, may hold values from -0.25 to 0.25
- weight_reduce: bfloat16 [2, 512, 512], replicated, may hold values from -0.25 to 0.25
Outputs:
- updated: bfloat16 [393216, 512], P(('wide', 'narrow'))
The draws below stay inside these ranges and needn't reach their ends.
Inputs may be any that keep to these rules, and one draw needn't show every extreme that they name: With e written as ((w * 16 + n) * 16 + s) * 96 + i, the reverse edge of e is ((s * 16 + n) * 16 + w) * 96 + reverse_position[e]; the reverse of the reverse is e, no edge is its own reverse, and the source atom of e is the target atom of its reverse. The target atom of an edge of device block w * 16 + n lies in atom block w * 16 + o (atom j in block j // 48), and route_slot = o * 192 + c with c distinct among the edges of one device block that have the same o. In every device block 192 edges have one o, none another o, and 96 each of the others; within each sub-block of the device block, 12 edges have that first o, none the second, and 6 each of the others. `atom_slots`: entry j * 32 + q, for atom j in block w * 16 + o, names the q-th incoming edge of j as n * 192 + c: the edge of device block w * 16 + n whose route_slot is o * 192 + c. Every atom has exactly 32 incoming edges, every edge is named once, and entries q from s * 2 to (s + 1) * 2 - 1 name edges of sub-block s.
All inputs are finite; a program needn't handle non-finite values.
Results may differ from the reference program's by a relative error of at most 0.015.
Values may be sent and summed in bfloat16 or wider, within the bound.
A program may use at most 128 MiB of HBM per device.

```python
import jax
import jax.numpy as jnp
from jax import lax

D = 512
SLOTS = 32
ATOM_DEV = 48
BLOCKS = 2
EDGE_DEV = 1536
COPIES = 2
SUBBLOCK = 96
CAP = 192
ATOMS = 12288
EDGES = 393216
N_WIDE = 16
N_NARROW = 16


def shuffled(key, shape):
    length = shape[-1]
    limit = 2147483647 // length
    scores = jax.random.randint(key, shape, 0, limit, dtype=jnp.int32) * length
    scores = scores + lax.broadcasted_iota(jnp.int32, shape, len(shape) - 1)
    return jnp.argsort(scores, axis=-1).astype(jnp.int32)


def build_graph(key):
    wide_count = N_WIDE
    narrow_count = N_NARROW
    sub_rows = SUBBLOCK
    device_rows = EDGE_DEV
    capacity = CAP
    share = sub_rows // narrow_count
    keys = jax.random.split(jax.random.fold_in(key, 271), 5)
    first_owner = shuffled(keys[0], (wide_count, narrow_count))
    second_owner = jnp.roll(first_owner, 1, axis=1)
    owner_ids = jnp.arange(narrow_count, dtype=jnp.int32)
    heavy = (owner_ids[None, None, :] == first_owner[:, :, None]).astype(jnp.int32)
    empty_pair = (owner_ids[None, None, :] == second_owner[:, :, None]).astype(jnp.int32)
    counts = share * (1 + heavy - empty_pair)
    piece_start = jnp.cumsum(counts, axis=1) - counts
    row_end = jnp.cumsum(counts, axis=2)
    row_start = row_end - counts
    positions = jnp.arange(sub_rows, dtype=jnp.int32)
    owner_at = jnp.sum((row_end[:, :, None, :] <= positions[None, None, :, None]).astype(jnp.int32), axis=3)
    start_at = jnp.take_along_axis(row_start, owner_at, axis=2)
    offset_at = jnp.take_along_axis(piece_start, owner_at, axis=2)
    item_pos = offset_at + positions[None, None, :] - start_at
    orders = shuffled(keys[1], (wide_count, wide_count, narrow_count, sub_rows))
    wide_ids = jnp.arange(wide_count, dtype=jnp.int32)[:, None, None, None]
    side_ids = jnp.arange(wide_count, dtype=jnp.int32)[None, None, :, None]
    items = orders[wide_ids, side_ids, owner_at[:, :, None, :], item_pos[:, :, None, :]]
    placing = shuffled(keys[2], (wide_count, narrow_count, wide_count, sub_rows))
    items = jnp.take_along_axis(items, placing, axis=3)
    owners = jnp.take_along_axis(jnp.broadcast_to(owner_at[:, :, None, :], items.shape), placing, axis=3)
    local_atom = items // COPIES
    copy_index = items % COPIES
    base_perm = shuffled(keys[3], (wide_count, narrow_count, wide_count, sub_rows))
    inverse_perm = jnp.argsort(base_perm, axis=3).astype(jnp.int32)
    mirrored = jnp.transpose(inverse_perm, (2, 1, 0, 3))
    paired = jnp.take_along_axis(base_perm, jnp.bitwise_xor(inverse_perm, 1), axis=3)
    row_wide = jnp.arange(wide_count, dtype=jnp.int32)[:, None, None, None]
    reverse_position = jnp.where(row_wide < side_ids, base_perm, jnp.where(row_wide > side_ids, mirrored, paired))
    flat_owner = owners.reshape(wide_count, narrow_count, device_rows)
    random_rank = shuffled(keys[4], (wide_count, narrow_count, device_rows))
    order_rows = jnp.argsort(flat_owner * device_rows + random_rank, axis=2).astype(jnp.int32)
    ranking = jnp.argsort(order_rows, axis=2).astype(jnp.int32)
    totals = counts * wide_count
    device_start = jnp.cumsum(totals, axis=2) - totals
    slot_rows = ranking - jnp.take_along_axis(device_start, flat_owner, axis=2)
    route_slot = flat_owner * capacity + slot_rows
    wide_three = jnp.arange(wide_count, dtype=jnp.int32)[:, None, None]
    narrow_three = jnp.arange(narrow_count, dtype=jnp.int32)[None, :, None]
    atom_index = (wide_three * narrow_count + flat_owner) * ATOM_DEV + local_atom.reshape(wide_count, narrow_count, device_rows)
    side_index = (jnp.arange(device_rows, dtype=jnp.int32) // sub_rows)[None, None, :]
    list_index = side_index * COPIES + copy_index.reshape(wide_count, narrow_count, device_rows)
    target_entry = atom_index * SLOTS + list_index
    entry_value = narrow_three * capacity + slot_rows
    atom_slots = jnp.zeros((EDGES,), jnp.int32).at[target_entry.reshape(-1)].set(entry_value.reshape(-1))
    return (reverse_position.reshape(-1), route_slot.reshape(-1), atom_slots)


def draw_reverse_position(key, part):
    return build_graph(key)[0]


def draw_route_slot(key, part):
    return build_graph(key)[1]


def draw_atom_slots(key, part):
    return build_graph(key)[2]


def block_levels(rng, dims, pieces, low, top_value):
    loudness = 1.0
    for dim, shards_of in pieces:
        draws = jax.random.uniform(jax.random.fold_in(jax.random.fold_in(rng, 6), dim), (shards_of,), jnp.float32, low / len(pieces), top_value / len(pieces))
        loudness = loudness * jnp.repeat(jnp.exp(draws), dims[dim] // shards_of).reshape((-1,) + (1,) * (len(dims) - 1 - dim))
    return loudness


def bell_draw(rng, dims, spread, most, shards=(), held_as=jnp.bfloat16):
    entries = spread * jax.random.normal(rng, dims, jnp.float32)
    if shards:
        entries = entries * block_levels(rng, dims, shards, -0.22, 0.18)
    return jnp.clip(entries, -most, most).astype(held_as)


def setup_inputs(seed: int = 0) -> dict:
    key_list = jax.random.split(jax.random.key(seed), 14)
    messages = bell_draw(key_list[0], (EDGES, D), 1.0, 6.0, ((0, 256),))
    reverse_position = draw_reverse_position(jax.random.fold_in(key_list[13], 71), 0)
    route_slot = draw_route_slot(jax.random.fold_in(key_list[13], 71), 0)
    atom_slots = draw_atom_slots(jax.random.fold_in(key_list[13], 71), 0)
    angles = bell_draw(key_list[4], (ATOMS, SLOTS * SLOTS), SLOTS ** -0.5, 1.0, ((0, 256),))
    weight_message = bell_draw(key_list[5], (BLOCKS, D, D), D ** -0.5, 0.25)
    weight_reverse = bell_draw(key_list[6], (BLOCKS, D, D), D ** -0.5, 0.25)
    weight_combine = bell_draw(key_list[7], (BLOCKS, D, D), D ** -0.5, 0.25)
    weight_inner = bell_draw(key_list[8], (BLOCKS, D, D), D ** -0.5, 0.25)
    weight_outer = bell_draw(key_list[9], (BLOCKS, D, D), D ** -0.5, 0.25)
    weight_lift = bell_draw(key_list[10], (BLOCKS, D, D), D ** -0.5, 0.25)
    weight_expand = bell_draw(key_list[11], (BLOCKS, D, D), D ** -0.5, 0.25)
    weight_reduce = bell_draw(key_list[12], (BLOCKS, D, D), D ** -0.5, 0.25)
    return dict(messages=messages, reverse_position=reverse_position, route_slot=route_slot, atom_slots=atom_slots, angles=angles, weight_message=weight_message, weight_reverse=weight_reverse, weight_combine=weight_combine, weight_inner=weight_inner, weight_outer=weight_outer, weight_lift=weight_lift, weight_expand=weight_expand, weight_reduce=weight_reduce)


ROOT_HALF = 0.7071067811865476


def project(operand, weight):
    return jnp.dot(operand, weight, preferred_element_type=jnp.float32)


def residual(previous, branch):
    return ((previous.astype(jnp.float32) + branch) * ROOT_HALF).astype(jnp.bfloat16)


def reverse_index(reverse_position):
    edge_ids = jnp.arange(EDGES, dtype=jnp.int32)
    block_rows = edge_ids // SUBBLOCK
    side_index = block_rows % N_WIDE
    narrow_index = (block_rows // N_WIDE) % N_NARROW
    wide_index = block_rows // (N_WIDE * N_NARROW)
    return ((side_index * N_NARROW + narrow_index) * N_WIDE + wide_index) * SUBBLOCK + reverse_position


def edge_lists(route_slot, atom_slots):
    edge_ids = jnp.arange(EDGES, dtype=jnp.int32)
    device_index = edge_ids // EDGE_DEV
    narrow_index = device_index % N_NARROW
    owner_block = device_index - narrow_index + route_slot // CAP
    table_key = owner_block * (N_NARROW * CAP) + narrow_index * CAP + route_slot % CAP
    edge_table = jnp.zeros((N_WIDE * N_NARROW * N_NARROW * CAP,), jnp.int32).at[table_key].set(edge_ids)
    entry_ids = jnp.arange(ATOMS * SLOTS, dtype=jnp.int32)
    atom_block = entry_ids // (SLOTS * ATOM_DEV)
    listed = edge_table[atom_block * (N_NARROW * CAP) + atom_slots]
    entry_of = jnp.zeros((EDGES,), jnp.int32).at[listed].set(entry_ids)
    return listed, entry_of


def mix_block(operands):
    return jnp.einsum("apq,aqd->apd", operands[0], operands[1].astype(jnp.float32),
                      precision=lax.Precision.HIGHEST).astype(jnp.bfloat16)


def reference(messages, reverse_position, route_slot, atom_slots, angles, weight_message, weight_reverse,
              weight_combine, weight_inner, weight_outer, weight_lift, weight_expand, weight_reduce):
    partner = reverse_index(reverse_position)
    listed, entry_of = edge_lists(route_slot, atom_slots)
    turn_rows = entry_of[partner]
    mixing = angles.astype(jnp.float32).reshape(N_WIDE * N_NARROW, ATOM_DEV, SLOTS, SLOTS)
    current = messages
    for section_index in range(BLOCKS):
        reverse = current[partner]
        hidden = jax.nn.silu(project(current, weight_message[section_index])
                             + project(reverse, weight_reverse[section_index])).astype(jnp.bfloat16)
        first_res = residual(current, project(hidden, weight_combine[section_index]))
        inner_value = jax.nn.silu(project(first_res, weight_inner[section_index])).astype(jnp.bfloat16)
        second = residual(first_res, jax.nn.silu(project(inner_value, weight_outer[section_index])))
        gathered = second[listed].reshape(N_WIDE * N_NARROW, ATOM_DEV, SLOTS, D)
        mixed_rows = lax.map(mix_block, (mixing, gathered)).reshape(EDGES, D)
        turned = mixed_rows[turn_rows]
        third_res = residual(second, jax.nn.silu(project(turned, weight_lift[section_index])))
        expand = jax.nn.silu(project(third_res, weight_expand[section_index])).astype(jnp.bfloat16)
        current = residual(third_res, jax.nn.silu(project(expand, weight_reduce[section_index])))
    return current
```

```python
import functools

import jax
import jax.numpy as jnp
from jax import lax
from jax.experimental import pallas as pl
from jax.experimental.pallas import tpu as pltpu
from jax.sharding import PartitionSpec as P

SLOTS = 32
BLOCKS = 2
N = 16
SUB = 96
CAP = 192
D = 512
GROUPS = 4
GR = 384
UNIT = 24
SHARE = 6
ROWS = 1536
ROOT_HALF = 0.7071067811865476
MESH = pl.DeviceIdType.MESH
F32 = jnp.float32
BF16 = jnp.bfloat16


def bit_xor(a, b):
    return 2 * ((a // 2 + b // 2) % 2) + (a % 2 + b % 2) % 2


def dot(a, b):
    return jnp.dot(a, b, preferred_element_type=F32)


def silu(v):
    return v / (1.0 + jnp.exp(-v))


def residual(previous, branch):
    return ((previous.astype(F32) + branch) * ROOT_HALF).astype(BF16)


def group(g, size=GR):
    return pl.ds(pl.multiple_of(g * size, 8), size)


def kernel(
    msg_hbm, rev_hbm, *rest
):
    weights_hbm = rest[:8]
    tables_hbm = rest[8:17]
    out_hbm = rest[17]
    (
        cur, rev, weights, mix, s0, s0t, sov, sovt, e_sel, e_selt, back_rows, p_f,
        second, mirror, x_buf, r_buf, y_buf, yb_buf, ret_buf, raw_buf,
        ov_buf, i_buf, o_buf, f_buf, out_buf,
        w_sem, t_sem, in_sem, out_sem,
        zs_sem, zr_sem, zl_sem, ws_sem, wr_sem, wl_sem,
        ps_sem, pr_sem, pl_sem, qs_sem, qr_sem, ql_sem,
    ) = rest[18:]
    tables = (mix, s0, s0t, sov, sovt, e_sel, e_selt, back_rows, p_f)

    w = lax.axis_index("wide")
    n = lax.axis_index("narrow")

    def side(beta):
        return 4 * bit_xor(w // 4, beta // 4) + bit_xor(w % 4, beta % 4)

    def msg_copy(beta):
        src = pl.ds(pl.multiple_of(side(beta) * SUB, 8), SUB)
        return pltpu.make_async_copy(msg_hbm.at[src], cur.at[group(beta, SUB)], in_sem.at[0, beta])

    def rev_copy(beta):
        src = pl.ds(pl.multiple_of(side(beta) * SUB, 8), SUB)
        return pltpu.make_async_copy(rev_hbm.at[src], rev.at[group(beta, SUB)], in_sem.at[1, beta])

    def weight_copy(k, b):
        return pltpu.make_async_copy(weights_hbm[k].at[b], weights.at[k, b], w_sem.at[k, b])

    def table_copy(k):
        return pltpu.make_async_copy(tables_hbm[k], tables[k], t_sem.at[k])

    def over(count, body):
        def step(i, carry):
            body(i)
            return carry

        lax.fori_loop(0, count, step, 0)

    def loads(beta):
        msg_copy(beta).start()
        rev_copy(beta).start()

    table_copy(7).start()
    over(N, loads)
    for k in range(5):
        weight_copy(k, 0).start()
    for k in (1, 3, 8, 6, 0, 5, 2, 4):
        table_copy(k).start()
    for k in range(5, 8):
        weight_copy(k, 0).start()
    for k in range(8):
        weight_copy(k, 1).start()
    f_buf[...] = jnp.zeros_like(f_buf)

    barrier = pltpu.get_barrier_semaphore()

    def greet(d):
        pl.semaphore_signal(barrier, 1, device_id={"narrow": (n + d + 1) % N}, device_id_type=MESH)
        pl.semaphore_signal(barrier, 1, device_id={"wide": (w + d + 1) % N}, device_id_type=MESH)

    over(N - 1, greet)
    pl.semaphore_wait(barrier, 2 * (N - 1))

    def z_copy(ex, src_buf, dst_buf, g, d, incoming):
        peer = (n + d) % N
        origin = (n + N - d) % N if incoming else n
        return pltpu.make_async_remote_copy(
            src_ref=src_buf.at[pl.ds(pl.multiple_of(g * GR + peer * UNIT, 8), UNIT)],
            dst_ref=dst_buf.at[pl.ds(pl.multiple_of(g * GR + origin * UNIT, 8), UNIT)],
            send_sem=zs_sem.at[ex, g, d],
            recv_sem=zr_sem.at[ex, g, d],
            device_id={"narrow": peer},
            device_id_type=MESH,
        )

    def z_local(ex, src_buf, dst_buf, g):
        rows = pl.ds(pl.multiple_of(g * GR + n * UNIT, 8), UNIT)
        return pltpu.make_async_copy(src_buf.at[rows], dst_buf.at[rows], zl_sem.at[ex, g])

    def z_send(ex, src_buf, dst_buf, g):
        def far(i):
            d = (8 + i) % N
            z_copy(ex, src_buf, dst_buf, g, d, False).start()

        def near(i):
            z_copy(ex, src_buf, dst_buf, g, 7 - i, False).start()

        over(8, far)
        over(7, near)
        z_local(ex, src_buf, dst_buf, g).start()

    def z_wait(ex, src_buf, dst_buf, g):
        over(N - 1, lambda i: z_copy(ex, src_buf, dst_buf, g, i + 1, True).wait_recv())
        z_local(ex, src_buf, dst_buf, g).wait()

    def w_copy(ex, src_buf, dst_buf, beta):
        rows = group(beta, SUB)
        return pltpu.make_async_remote_copy(
            src_ref=src_buf.at[rows],
            dst_ref=dst_buf.at[rows],
            send_sem=ws_sem.at[ex, beta],
            recv_sem=wr_sem.at[ex, beta],
            device_id={"wide": side(beta)},
            device_id_type=MESH,
        )

    def w_local(ex, src_buf, dst_buf):
        return pltpu.make_async_copy(src_buf.at[pl.ds(0, SUB)], dst_buf.at[pl.ds(0, SUB)], wl_sem.at[ex])

    def w_send(ex, src_buf, dst_buf, g):
        def one(b):
            beta = 4 * g + b

            @pl.when(beta > 0)
            def _():
                w_copy(ex, src_buf, dst_buf, beta).start()

            @pl.when(beta == 0)
            def _():
                w_local(ex, src_buf, dst_buf).start()

        over(4, one)

    def w_wait(ex, src_buf, dst_buf, g):
        def one(b):
            beta = 4 * g + b

            @pl.when(beta > 0)
            def _():
                w_copy(ex, src_buf, dst_buf, beta).wait_recv()

            @pl.when(beta == 0)
            def _():
                w_local(ex, src_buf, dst_buf).wait()

        over(4, one)

    def p_copy(ph, g, cc):
        j = 4 * cc + g
        return pltpu.make_async_remote_copy(
            src_ref=ov_buf.at[ph, group(g, UNIT), pl.ds(pl.multiple_of(cc * 128, 128), 128)],
            dst_ref=i_buf.at[ph, group(n, UNIT)],
            send_sem=ps_sem.at[ph, j],
            recv_sem=pr_sem.at[ph, n],
            device_id={"narrow": j},
            device_id_type=MESH,
        )

    def p_local(ph, g, cc):
        return pltpu.make_async_copy(
            ov_buf.at[ph, group(g, UNIT), pl.ds(pl.multiple_of(cc * 128, 128), 128)],
            i_buf.at[ph, group(n, UNIT)],
            pl_sem.at[ph],
        )

    def p_arrival(ph, m):
        return pltpu.make_async_remote_copy(
            src_ref=ov_buf.at[ph, pl.ds(0, UNIT), pl.ds(0, 128)],
            dst_ref=i_buf.at[ph, group(m, UNIT)],
            send_sem=ps_sem.at[ph, m],
            recv_sem=pr_sem.at[ph, m],
            device_id={"narrow": m},
            device_id_type=MESH,
        )

    def p_send(ph, g):
        def one(cc):
            j = 4 * cc + g

            @pl.when(j != n)
            def _():
                p_copy(ph, g, cc).start()

            @pl.when(j == n)
            def _():
                p_local(ph, g, cc).start()

        over(4, one)

    def q_copy(ph, d):
        t = (n + d) % N
        g, cc = n % 4, n // 4
        return pltpu.make_async_remote_copy(
            src_ref=o_buf.at[ph, group(t, UNIT)],
            dst_ref=f_buf.at[ph, pl.ds(pl.multiple_of(g * 128, 128), UNIT), pl.ds(pl.multiple_of(cc * 128, 128), 128)],
            send_sem=qs_sem.at[ph, d],
            recv_sem=qr_sem.at[ph, n],
            device_id={"narrow": t},
            device_id_type=MESH,
        )

    def q_local(ph):
        g, cc = n % 4, n // 4
        return pltpu.make_async_copy(
            o_buf.at[ph, group(n, UNIT)],
            f_buf.at[ph, pl.ds(pl.multiple_of(g * 128, 128), UNIT), pl.ds(pl.multiple_of(cc * 128, 128), 128)],
            ql_sem.at[ph],
        )

    def q_arrival(ph, g, cc):
        j = 4 * cc + g
        return pltpu.make_async_remote_copy(
            src_ref=o_buf.at[ph, pl.ds(0, UNIT)],
            dst_ref=f_buf.at[ph, pl.ds(pl.multiple_of(g * 128, 128), UNIT), pl.ds(pl.multiple_of(cc * 128, 128), 128)],
            send_sem=qs_sem.at[ph, j],
            recv_sem=qr_sem.at[ph, j],
            device_id={"narrow": j},
            device_id_type=MESH,
        )

    def forward_surplus(ph, g, turned_back):
        @pl.when(n % 4 == g)
        def _():
            over(N - 1, lambda i: p_arrival(ph, (n + i + 1) % N).wait_recv())
            p_local(ph, n % 4, n // 4).wait()
            lines = i_buf[ph]
            if turned_back:
                moved = lax.dot_general(p_f[...], lines, (((0,), (0,)), ((), ())), preferred_element_type=F32)
            else:
                moved = dot(p_f[...], lines)
            o_buf[ph] = moved.astype(BF16)
            over(N - 1, lambda i: q_copy(ph, i + 1).start())
            q_local(ph).start()

    def wait_surplus(ph, g):
        def one(cc):
            j = 4 * cc + g

            @pl.when(j != n)
            def _():
                q_arrival(ph, g, cc).wait_recv()

            @pl.when(j == n)
            def _():
                q_local(ph).wait()

        over(4, one)

    def front(b, current, reverse):
        hidden = silu(dot(current, weights[0, b]) + dot(reverse, weights[1, b])).astype(BF16)
        first = residual(current, dot(hidden, weights[2, b]))
        inner = silu(dot(first, weights[3, b])).astype(BF16)
        return residual(first, silu(dot(inner, weights[4, b])))

    def back(b, second_rows, turned):
        third = residual(second_rows, silu(dot(turned, weights[5, b])))
        expand = silu(dot(third, weights[6, b])).astype(BF16)
        return residual(third, silu(dot(expand, weights[7, b])))

    def edge_order(g, raw):
        return dot(back_rows[group(g)], raw[group(g)]).astype(BF16)

    def stage_front(b, g, current, reverse):
        value = front(b, current, reverse)
        second[b, group(g)] = value
        if b == 0:
            w_send(0, second.at[0], mirror, g)
        ov_buf[2 * b, group(g, UNIT)] = dot(sov[group(g, UNIT)], value).astype(BF16)
        p_send(2 * b, g)

    def stage_out(b, g):
        wait_surplus(2 * b, g)
        rows = dot(s0[group(g)], second[b, group(g)]) + dot(e_selt[...], f_buf[2 * b, group(g, 128)])
        x_buf[b, group(g)] = rows.astype(BF16)
        z_send(2 * b, x_buf.at[b], r_buf.at[b], g)

    def stage_mix(b, g):
        y_buf[b, group(g)] = dot(mix[group(g)], r_buf[b]).astype(BF16)
        z_send(2 * b + 1, y_buf.at[b], yb_buf.at[b], g)

    def stage_returned(b, g):
        z_wait(2 * b + 1, y_buf.at[b], yb_buf.at[b], g)
        ov_buf[2 * b + 1, group(g, UNIT)] = dot(e_sel[...], yb_buf[b, group(g)]).astype(BF16)
        p_send(2 * b + 1, g)

    def stage_wide(b, g):
        wait_surplus(2 * b + 1, g)
        rows = dot(s0t[group(g)], yb_buf[b, group(g)]) + dot(sovt[group(g)], f_buf[2 * b + 1, group(g, 128)])
        ret_buf[b, group(g)] = rows.astype(BF16)
        w_send(1 + b, ret_buf.at[b], raw_buf.at[b], g)

    def staged(step, stages):
        for lag, stage in reversed(list(enumerate(stages))):
            g = step - lag

            @pl.when((g >= 0) & (g < GROUPS))
            def _(stage=stage, g=g):
                stage(g)

    table_copy(7).wait()
    for k in range(5):
        weight_copy(k, 0).wait()
    for k in (1, 3, 8, 6):
        table_copy(k).wait()

    def start_front(g):
        def landed(b):
            msg_copy(4 * g + b).wait()
            rev_copy(4 * g + b).wait()

        over(4, landed)
        stage_front(0, g, cur[group(g)], edge_order(g, rev))

    over(GROUPS + 2, lambda step: staged(step, (
        start_front,
        lambda g: forward_surplus(0, g, False),
        lambda g: stage_out(0, g),
    )))

    for k in (0, 5, 2, 4):
        table_copy(k).wait()
    for k in range(5, 8):
        weight_copy(k, 0).wait()
    for k in range(8):
        weight_copy(k, 1).wait()

    over(GROUPS, lambda g: z_wait(0, x_buf.at[0], r_buf.at[0], g))
    over(GROUPS, lambda g: stage_mix(0, g))

    def middle(g):
        w_wait(1, ret_buf.at[0], raw_buf.at[0], g)
        w_wait(0, second.at[0], mirror, g)
        turned = edge_order(g, raw_buf.at[0])
        current = back(0, second[0, group(g)], turned)
        reverse = back(0, edge_order(g, mirror), ret_buf[0, group(g)])
        stage_front(1, g, current, reverse)

    over(GROUPS + 5, lambda step: staged(step, (
        lambda g: stage_returned(0, g),
        lambda g: forward_surplus(1, g, True),
        lambda g: stage_wide(0, g),
        middle,
        lambda g: forward_surplus(2, g, False),
        lambda g: stage_out(1, g),
    )))

    over(GROUPS, lambda g: z_wait(2, x_buf.at[1], r_buf.at[1], g))
    over(GROUPS, lambda g: stage_mix(1, g))

    def out_copy(beta):
        dst = pl.ds(pl.multiple_of(side(beta) * SUB, 8), SUB)
        return pltpu.make_async_copy(out_buf.at[group(beta, SUB)], out_hbm.at[dst], out_sem.at[beta])

    def last(g):
        w_wait(2, ret_buf.at[1], raw_buf.at[1], g)
        out_buf[group(g)] = back(1, second[1, group(g)], edge_order(g, raw_buf.at[1]))
        over(4, lambda b: out_copy(4 * g + b).start())

    over(GROUPS + 3, lambda step: staged(step, (
        lambda g: stage_returned(1, g),
        lambda g: forward_surplus(3, g, True),
        lambda g: stage_wide(1, g),
        last,
    )))

    over(N, lambda beta: out_copy(beta).wait())
    for ex, (src_buf, dst_buf) in enumerate((
        (x_buf.at[0], r_buf.at[0]), (y_buf.at[0], yb_buf.at[0]),
        (x_buf.at[1], r_buf.at[1]), (y_buf.at[1], yb_buf.at[1]),
    )):
        def drain(g, ex=ex, src_buf=src_buf, dst_buf=dst_buf):
            over(N - 1, lambda i: z_copy(ex, src_buf, dst_buf, g, i + 1, False).wait_send())

        over(GROUPS, drain)
    for ex, (src_buf, dst_buf) in enumerate((
        (second.at[0], mirror), (ret_buf.at[0], raw_buf.at[0]), (ret_buf.at[1], raw_buf.at[1]),
    )):
        over(N - 1, lambda i, ex=ex, s=src_buf, d=dst_buf: w_copy(ex, s, d, i + 1).wait_send())
    for ph in range(4):
        def drain_p(j, ph=ph):
            @pl.when(j != n)
            def _():
                p_copy(ph, j % 4, j // 4).wait_send()

        over(N, drain_p)
        over(N - 1, lambda i, ph=ph: q_copy(ph, i + 1).wait_send())


def one_hot(index, size):
    return (index[..., None] == jnp.arange(size, dtype=jnp.int32)).astype(BF16)


def one_hot_rows(index, size):
    return (index[..., None, :] == jnp.arange(size, dtype=jnp.int32)[:, None]).astype(BF16)


def tables_of(reverse_position, route_slot, atom_slots, angles):
    w = lax.axis_index("wide")
    sides = jnp.bitwise_xor(w, jnp.arange(N, dtype=jnp.int32))
    betas = jnp.arange(N, dtype=jnp.int32)

    route = route_slot.reshape(N, SUB)[sides]
    place = reverse_position.reshape(N, SUB)[sides]
    owner = route // CAP
    same = owner[:, :, None] == owner[:, None, :]
    rank = jnp.sum((same & (route[:, None, :] < route[:, :, None])).astype(jnp.int32), axis=2)
    counts = jnp.sum((owner[0][:, None] == jnp.arange(N, dtype=jnp.int32)).astype(jnp.int32), axis=0)
    heavy = jnp.argmax(counts).astype(jnp.int32)
    empty = jnp.argmin(counts).astype(jnp.int32)
    surplus = rank >= SHARE
    column = (betas % 4)[:, None] * SHARE
    direct = jnp.where(surplus, -1, owner * UNIT + column + rank).reshape(GROUPS, GR)
    extra = jnp.where(surplus, column + rank - SHARE, -1).reshape(GROUPS, GR)
    s0 = one_hot_rows(direct, GR).reshape(ROWS, GR)
    s0t = one_hot(direct, GR).reshape(ROWS, GR)
    sov = one_hot_rows(extra, UNIT).reshape(GROUPS * UNIT, GR)
    sovt = one_hot(extra, 128).reshape(ROWS, 128)
    spot = empty * UNIT + jnp.arange(UNIT, dtype=jnp.int32)
    e_sel = one_hot(spot, GR)
    lane = jnp.arange(GR, dtype=jnp.int32) - empty * UNIT
    e_selt = one_hot(jnp.where((lane >= 0) & (lane < UNIT), lane, -1), 128)
    in_group = (betas % 4)[:, None] * SUB + place
    back_rows = one_hot(in_group.reshape(GROUPS, GR), GR).reshape(ROWS, GR)

    pairs = lax.all_gather(jnp.stack([heavy, empty]), "narrow", axis=0, tiled=False)
    heavies, empties = pairs[:, 0], pairs[:, 1]
    before = jnp.arange(N)[:, None] > jnp.arange(N)[None, :]
    heavy_rank = jnp.sum(((heavies[:, None] == heavies[None, :]) & before).astype(jnp.int32), axis=1)
    empty_rank = jnp.sum(((empties[:, None] == empties[None, :]) & before).astype(jnp.int32), axis=1)
    carries = (heavies[:, None] == empties[None, :]) & (heavy_rank[:, None] == empty_rank[None, :])
    ids = jnp.arange(N, dtype=jnp.int32)
    carrier = jnp.sum(jnp.where(carries, ids[None, :], 0), axis=1)
    source = jnp.sum(jnp.where(carries, ids[:, None], 0), axis=0)
    lines = jnp.arange(N * UNIT, dtype=jnp.int32)
    p_f = one_hot(source[lines // UNIT] * UNIT + lines % UNIT, GR)

    atoms = angles.shape[0]
    entry = atom_slots.reshape(atoms, N, 2).transpose(1, 0, 2).reshape(N, 2 * atoms)
    origin = entry // CAP
    same = origin[:, :, None] == origin[:, None, :]
    rank = jnp.sum((same & (entry[:, None, :] < entry[:, :, None])).astype(jnp.int32), axis=2)
    by = jnp.sum(jnp.where(origin[..., None] == ids, carrier, 0), axis=-1)
    beta = jnp.bitwise_xor(w, jnp.arange(N, dtype=jnp.int32))[:, None]
    spot = jnp.where(rank < SHARE, origin * UNIT + rank, by * UNIT + rank - SHARE)
    spot = spot + (beta // 4) * GR + (beta % 4) * SHARE
    spot = spot.reshape(N, atoms, 2).transpose(1, 0, 2).reshape(atoms, SLOTS)
    picked = one_hot(spot, ROWS)
    mixing = angles.reshape(atoms, SLOTS, SLOTS)
    spread = jnp.einsum("apq,aqx->apx", mixing, picked, preferred_element_type=F32).astype(BF16)
    put = one_hot_rows(spot.reshape(-1), ROWS)
    mix = dot(put, spread.reshape(ROWS, ROWS)).astype(BF16)
    return mix, s0, s0t, sov, sovt, e_sel, e_selt, back_rows, p_f


def local(messages, reverse_position, route_slot, atom_slots, angles, *weights):
    raw = lax.all_to_all(messages, "wide", split_axis=0, concat_axis=0, tiled=True)
    tables = tables_of(reverse_position, route_slot, atom_slots, angles)
    vm = pltpu.VMEM
    dma = pltpu.SemaphoreType.DMA
    rows = (ROWS, D)
    scratch = [
        vm(rows, BF16), vm(rows, BF16), vm((8, 2, D, D), BF16),
        *[vm(t.shape, BF16) for t in tables],
        vm((2, *rows), BF16), vm(rows, BF16),
        *[vm((2, *rows), BF16) for _ in range(6)],
        vm((4, GROUPS * UNIT, D), BF16), vm((4, GR, 128), BF16), vm((4, GR, 128), BF16),
        vm((4, GROUPS * 128, D), BF16), vm(rows, BF16),
        dma((8, 2)), dma((9,)), dma((2, N)), dma((N,)),
        dma((4, GROUPS, N)), dma((4, GROUPS, N)), dma((4, GROUPS)),
        dma((3, N)), dma((3, N)), dma((3,)),
        dma((4, N)), dma((4, N)), dma((4,)), dma((4, N)), dma((4, N)), dma((4,)),
    ]
    any_space = pl.BlockSpec(memory_space=pl.ANY)
    return pl.pallas_call(
        kernel,
        out_shape=jax.ShapeDtypeStruct(rows, BF16),
        in_specs=[any_space] * (2 + 8 + 9),
        out_specs=any_space,
        scratch_shapes=scratch,
        compiler_params=pltpu.CompilerParams(
            collective_id=0, has_side_effects=True, vmem_limit_bytes=66 * 1024 * 1000
        ),
        name="triplets",
    )(messages, raw, *weights, *tables)


def solution(mesh):
    split = P(("wide", "narrow"), None)
    flat = P(("wide", "narrow"))
    in_specs = (split, flat, flat, flat, split) + (P(),) * 8
    return jax.shard_map(local, mesh=mesh, in_specs=in_specs, out_specs=split, check_vma=False)
```
